32 devices in a mesh: dp: 2 (over y), expert: 16 (over z, x, core).
Axes of the slice: x: 2, y: 2, z: 4, core: 2. Of those that a mesh axis runs over, the one named last changes fastest.
Arguments:
- out_grad: bfloat16 [768, 7168], P('expert', 'dp'), may hold values from -6 to 6
- gate_weight: float32 [768, 8], P('expert'), may hold values from 0.05 to 0.5
- expert_ids: int32 [768, 8], P('expert'), may hold values from 0 to 15, all different within a row; in each aligned block of 48 rows (0 to 47, 48 to 95, ...) at most 36 rows name the same one
- replicated: int32 [16], replicated, may hold values from 0 to 1, as said below
- down_weight: bfloat16 [16, 1024, 7168], P('expert', None, 'dp'), may hold values from -0.0625 to 0.0625
- pre_act: bfloat16 [16, 2, 576, 2048], P('expert', None, 'dp'), may hold values from -6 to 6
Outputs:
- grad_down: bfloat16 [16, 1024, 7168], P('expert', None, 'dp')
- grad_pre: bfloat16 [16, 2, 576, 2048], P('expert', None, 'dp')
The draws below stay inside these ranges and needn't reach their ends.
Inputs may be any that keep to these rules, and one draw needn't show every extreme that they name: `expert_ids`: each row names 8 different experts; among the 48 rows of one device no expert is named more than 36 times, a bound that some block reaches. `replicated`: expert 0 always has a redundant slot; each other expert has one with chance one half.
All inputs are finite; a program needn't handle non-finite values.
Results may differ from the reference program's by a relative error of at most 0.018.
Values may be sent and summed in bfloat16 or wider, within the bound.
No kernel may reach another device: no remote copies, remote signals or barrier semaphores. Data moves between devices by JAX's collectives and lax.ppermute only.
A program may use at most 64 MiB of HBM per device.

```python
import math
import jax
import jax.numpy as jnp
import numpy as np
from jax import lax

D = 7168
TOPK = 8
F = 1024
TOK_DEV = 48
TOKENS = 768
CAP = 36
ROWS = 576
N_DP = 2
N_EXPERT = 16


def draw_replicated(key, part):
    flags = jax.random.randint(jax.random.fold_in(key, 7), (N_EXPERT,), 0, 2).astype(jnp.int32)
    return flags.at[0].set(1)


def block_levels(key, extent, shards, smallest, top_value):
    def one(axis_at, parts):
        heights = jax.random.uniform(jax.random.fold_in(jax.random.fold_in(key, 6), axis_at), (parts,), jnp.float32, smallest / len(shards), top_value / len(shards))
        return jnp.repeat(jnp.exp(heights), extent[axis_at] // parts).reshape((-1,) + (1,) * (len(extent) - axis_at - 1))

    gain = one(*shards[0])
    for cut in shards[1:]:
        gain = gain * one(*cut)
    return gain


def assign_block(rng, own, number, rows, number_of, top, most, skew):
    ranking = jax.random.permutation(rng, number_of)
    packed, common = shares(number_of, rows * top, most, skew, True), shares(number_of, rows * top, most, skew, False)
    places = jnp.arange(number_of)

    def named(lengths, rotation):
        used = int((lengths > 0).sum())
        fixed = max(1, used // 4)
        moved = fixed + (places - fixed + rotation * (used - fixed)) % max(1, number_of - fixed)
        return jnp.zeros((number_of,), jnp.int32).at[ranking[jnp.where(places < fixed, places, moved)]].set(jnp.asarray(lengths, jnp.int32))

    lengths = jnp.where(number % 4 == 0, named(packed, number // 4), named(common, number - number // 4 - 1))
    mixed = jax.random.permutation(jax.random.fold_in(own, 3), number_of)
    giver, sink = mixed[0:number_of // 2 * 2:2], mixed[1:number_of // 2 * 2:2]
    margin = jnp.minimum(lengths[giver] - 1, most - lengths[sink]) // 2
    margin = jnp.where((giver == ranking[0]) | (sink == ranking[0]) | (lengths[sink] == 0), 0, jnp.maximum(margin, 0))
    moved = jax.random.randint(jax.random.fold_in(own, 4), (number_of // 2,), 0, 1 << 20) % (margin + 1)
    lengths = lengths.at[giver].add(-moved).at[sink].add(moved)
    items = jnp.searchsorted(jnp.cumsum(lengths), jnp.arange(rows * top), side="right").astype(jnp.int32)
    grid = items.reshape(top, rows).T
    grid = grid[jax.random.permutation(jax.random.fold_in(own, 1), rows)]
    rotation = jax.random.randint(jax.random.fold_in(own, 2), (rows, 1), 0, top)
    return jnp.take_along_axis(grid, (jnp.arange(top)[None, :] + rotation) % top, axis=1)


def shares(count, total, bound, skew, full):
    loads = [(1 << 20) // math.isqrt(grade ** skew) + 1 for grade in range(1, count + 1)]
    largest = bound if full else min(bound, max(-(-total // count), total * loads[0] // sum(loads)))
    least = 1 if total - largest >= count - 1 else 0
    given, rest = [largest] + [least] * (count - 1), total - largest - least * (count - 1)
    while rest > 0:
        free = [i for i in range(1, count) if given[i] < largest] or [i for i in range(1, count) if given[i] < bound]
        whole, remaining = sum([loads[i] for i in free]), rest
        for i in free:
            extra = min(bound - given[i], max(1, remaining * loads[i] // whole), rest)
            given[i] = given[i] + extra
            rest = rest - extra
    return np.array(given)


def bell_draw(key, shape, spread, most, shards=(), held_as=jnp.bfloat16):
    gain = block_levels(key, shape, shards, -0.22, 0.18) if shards else 1.0
    result = jax.random.normal(key, shape, jnp.float32) * spread * gain
    return jnp.minimum(jnp.maximum(result, -most), most).astype(held_as)


def setup_inputs(seed: int = 0) -> dict:
    key_of = jax.random.split(jax.random.key(seed), 7)
    out_grad = bell_draw(key_of[0], (TOKENS, D), 1.0, 6.0, ((0, 16), (1, 2)))
    gate_weight = jnp.clip(jnp.exp(math.log(0.5) - 2.3025851 * jax.random.uniform(key_of[1], (TOKENS, TOPK), jnp.float32) ** block_levels(key_of[1], (TOKENS, TOPK), ((0, 16),), -0.2, 0.2)), 0.05, 0.5)
    expert_ids_keys = jax.random.split(jax.random.fold_in(key_of[2], 1), TOKENS // TOK_DEV)
    expert_ids_turns = jax.random.permutation(jax.random.fold_in(key_of[2], 3), TOKENS // TOK_DEV)
    expert_ids = jax.vmap(lambda own, number: assign_block(jax.random.fold_in(key_of[2], 2), own, number, TOK_DEV, N_EXPERT, TOPK, CAP, 1))(expert_ids_keys, expert_ids_turns).reshape((TOKENS, TOPK))
    replicated = draw_replicated(jax.random.fold_in(key_of[6], 71), 0)
    down_weight = bell_draw(key_of[4], (N_EXPERT, F, D), D ** -0.5, 0.0625, ((0, 16), (2, 2)))
    pre_act = bell_draw(key_of[5], (N_EXPERT, 2, ROWS, 2 * F), 1.0, 6.0, ((0, 16), (2, 2)))
    return dict(out_grad=out_grad, gate_weight=gate_weight, expert_ids=expert_ids, replicated=replicated, down_weight=down_weight, pre_act=pre_act)


def hidden_of(stored):
    width = stored.shape[-1] // 2
    gate_part = stored[..., :width].astype(jnp.float32)
    up_part = stored[..., width:].astype(jnp.float32)
    return (gate_part * jax.nn.sigmoid(gate_part) * up_part).astype(jnp.bfloat16)


def swiglu_back(hidden_grad, stored):
    width = stored.shape[-1] // 2
    gate_part = stored[..., :width].astype(jnp.float32)
    up_part = stored[..., width:].astype(jnp.float32)
    sigmoid_v = jax.nn.sigmoid(gate_part)
    gate_grad = hidden_grad * up_part * sigmoid_v * (1.0 + gate_part * (1.0 - sigmoid_v))
    up_grad = hidden_grad * gate_part * sigmoid_v
    return jnp.concatenate([gate_grad, up_grad], axis=-1).astype(jnp.bfloat16)


def width_sum(rows, weight):
    block = D // N_DP
    left = rows.astype(jnp.float32).reshape(rows.shape[0], N_DP, block)
    right = weight.astype(jnp.float32).reshape(weight.shape[0], N_DP, block)
    terms = jnp.einsum("rnd,fnd->nrf", left, right, precision=lax.Precision.HIGHEST)
    rounded = lax.optimization_barrier(terms.astype(jnp.bfloat16)).astype(jnp.float32)
    return jnp.sum(rounded, axis=0)


def reference(out_grad, gate_weight, expert_ids, replicated, down_weight, pre_act):
    half_way = N_EXPERT // 2
    route_ids = expert_ids.reshape(N_EXPERT, TOK_DEV * TOPK)
    experts_iota = jnp.arange(N_EXPERT, dtype=jnp.int32)
    onehot = (route_ids[:, :, None] == experts_iota[None, None, :]).astype(jnp.int32)
    position = jnp.sum(onehot * (jnp.cumsum(onehot, axis=1) - 1), axis=2).astype(jnp.int32)
    source = jnp.broadcast_to(experts_iota[:, None], route_ids.shape)
    rep_of = replicated[route_ids]
    diverted = (rep_of == 1) & (source % 2 == 1)
    target_dev = jnp.where(diverted, (route_ids + half_way) % N_EXPERT, route_ids).reshape(-1)
    slot_index = diverted.astype(jnp.int32)
    flat_index = (slot_index * ROWS + source * CAP + position).reshape(-1).astype(jnp.int32)
    scaled = gate_weight.reshape(-1)[:, None] * jnp.repeat(out_grad.astype(jnp.float32), TOPK, axis=0)
    routed = scaled.astype(jnp.bfloat16)

    def dispatch_for(device):
        scatter_index = jnp.where(target_dev == device, flat_index, 2 * ROWS).astype(jnp.int32)
        buffer = jnp.zeros((2 * ROWS, D), routed.dtype).at[scatter_index].set(routed, mode="drop")
        return buffer.reshape(2, ROWS, D)

    def per_expert(expert):
        partner = ((expert + half_way) % N_EXPERT).astype(jnp.int32)
        own_rows = dispatch_for(expert)
        theirs = dispatch_for(partner)[1]
        own_weight = down_weight[expert]
        rep_weight = down_weight[partner]
        grad_own = width_sum(own_rows[0], own_weight)
        grad_rep = width_sum(own_rows[1], rep_weight)
        stored = pre_act[expert]
        pre_own = swiglu_back(grad_own, stored[0])
        pre_rep = swiglu_back(grad_rep, stored[1])
        hidden_own = hidden_of(stored[0])
        hidden_rep = hidden_of(pre_act[partner, 1])
        weight_grad = jnp.dot(hidden_own.T, own_rows[0], preferred_element_type=jnp.float32)
        weight_grad = weight_grad + jnp.dot(hidden_rep.T, theirs, preferred_element_type=jnp.float32)
        return weight_grad.astype(jnp.bfloat16), jnp.stack([pre_own, pre_rep])

    grad_down, grad_pre = lax.map(per_expert, experts_iota)
    return grad_down, grad_pre
```

```python
import functools

import jax
import jax.numpy as jnp
from jax import lax
from jax.experimental import pallas as pl
from jax.experimental.pallas import tpu as pltpu
from jax.sharding import PartitionSpec as P


LANES = 128
FIELDS = 4


def swapped(value, axis, mask):
    count = lax.axis_size(axis)
    return lax.ppermute(value, axis, [(s, s ^ mask) for s in range(count)])


def passed_along(value, axis, steps):
    count = lax.axis_size(axis)
    pairs = [(source, (source + steps) % count) for source in range(count)]
    return lax.ppermute(value, axis, pairs)


def hidden_of(stored):
    width = stored.shape[-1] // 2
    gate_part = stored[..., :width].astype(jnp.float32)
    up_part = stored[..., width:].astype(jnp.float32)
    return (gate_part * jax.nn.sigmoid(gate_part) * up_part).astype(jnp.bfloat16)


def swiglu_back(hidden_grad, stored):
    width = stored.shape[-1] // 2
    gate_part = stored[..., :width].astype(jnp.float32)
    up_part = stored[..., width:].astype(jnp.float32)
    sigmoid_v = jax.nn.sigmoid(gate_part)
    gate_grad = hidden_grad * up_part * sigmoid_v * (1.0 + gate_part * (1.0 - sigmoid_v))
    up_grad = hidden_grad * gate_part * sigmoid_v
    return jnp.concatenate([gate_grad, up_grad], axis=-1).astype(jnp.bfloat16)


def payload_body(ids_ref, weight_ref, grad_ref, out_ref, *, experts, width):
    tokens = grad_ref.shape[0]
    meta = out_ref.shape[1] - width
    lane = lax.broadcasted_iota(jnp.int32, (tokens, meta), 1)
    expert, field = lane % experts, lane // experts
    ids = jnp.transpose(ids_ref[...])
    weight = jnp.transpose(weight_ref[...])
    named = jnp.zeros((tokens, meta), jnp.float32)
    chosen = jnp.zeros((tokens, meta), jnp.float32)
    for k in range(ids.shape[1]):
        hit = ids[:, k : k + 1] == expert
        named = jnp.where(hit, 1.0, named)
        chosen = jnp.where(hit, weight[:, k : k + 1], chosen)
    rows = lax.broadcasted_iota(jnp.int32, (tokens, tokens), 0)
    cols = lax.broadcasted_iota(jnp.int32, (tokens, tokens), 1)
    earlier = (cols < rows).astype(jnp.bfloat16)
    position = jnp.dot(earlier, named.astype(jnp.bfloat16), preferred_element_type=jnp.float32)
    top = chosen.astype(jnp.bfloat16).astype(jnp.float32)
    mid = (chosen - top).astype(jnp.bfloat16).astype(jnp.float32)
    low = chosen - top - mid
    place = jnp.where(named > 0.0, position, -1.0)
    value = jnp.where(field == 0, place, jnp.where(field == 1, top, jnp.where(field == 2, mid, low)))
    value = jnp.where(field < FIELDS, value, 0.0)
    out_ref[:, :width] = grad_ref[...]
    out_ref[:, width:] = value.astype(jnp.bfloat16)


def payload_of(out_grad, gate_weight, expert_ids, experts):
    tokens, width = out_grad.shape
    meta = -(-experts * FIELDS // LANES) * LANES
    return pl.pallas_call(
        functools.partial(payload_body, experts=experts, width=width),
        out_shape=jax.ShapeDtypeStruct((tokens, width + meta), jnp.bfloat16),
        name="payload",
    )(expert_ids.T, gate_weight.T, out_grad)


def chunk_body(info, *refs, experts, capacity, aliased):
    data, meta = refs[:4], refs[4:8]
    weight = refs[8]
    merged_ref, partial_ref, pick_ref, scale_ref, stack_ref, acc_ref = refs[9 + aliased :]
    tokens = data[0].shape[0]
    total = 4 * tokens
    rows = merged_ref.shape[0]
    step = pl.program_id(0)
    myself = info[0]

    @pl.when(step == 0)
    def _():
        width = meta[0].shape[1]
        lane = lax.broadcasted_iota(jnp.int32, (tokens, width), 1)
        row = lax.broadcasted_iota(jnp.int32, (tokens, rows), 1)
        seen = jnp.zeros((rows, width), jnp.float32)
        for i in range(4):
            values = meta[i][...]
            place = jnp.sum(
                jnp.where(lane == myself, values.astype(jnp.float32), 0.0), axis=1, keepdims=True
            ).astype(jnp.int32)
            target = jnp.where(place >= 0, place + info[2 + i], -1)
            pick = (target == row).astype(jnp.float32).astype(jnp.bfloat16)
            pick_ref[i * tokens : (i + 1) * tokens, :] = pick
            seen = seen + lax.dot_general(
                pick, values, (((0,), (0,)), ((), ())), preferred_element_type=jnp.float32
            )
        lane = lax.broadcasted_iota(jnp.int32, (rows, width), 1)
        wanted = (lane % experts == myself) & (lane >= experts) & (lane < FIELDS * experts)
        scale = jnp.sum(jnp.where(wanted, seen, 0.0), axis=1, keepdims=True)
        scale_ref[...] = jnp.broadcast_to(scale, scale_ref.shape)
        acc_ref[...] = jnp.zeros_like(acc_ref)

    for i in range(4):
        stack_ref[i * tokens : (i + 1) * tokens, :] = data[i][...]
    chosen = lax.dot_general(
        pick_ref[...], stack_ref[...], (((0,), (0,)), ((), ())), preferred_element_type=jnp.float32
    )
    merged = (scale_ref[:, :1] * chosen).astype(jnp.bfloat16)
    merged_ref[...] = merged
    acc_ref[...] += lax.dot_general(
        merged, weight[...], (((1,), (1,)), ((), ())), preferred_element_type=jnp.float32
    )

    @pl.when(step == pl.num_programs(0) - 1)
    def _():
        partial_ref[...] = acc_ref[...].astype(jnp.bfloat16)


def chunk_of(info, shards, weight, merged, experts, capacity, all_rows, tile):
    tokens = shards[0].shape[0]
    hidden, width = weight.shape
    rows = 4 * capacity
    meta = shards[0].shape[1] - width
    aliased = int(merged is not None)
    in_specs = [pl.BlockSpec((tokens, tile), lambda j, info: (0, j)) for _ in range(4)]
    in_specs += [pl.BlockSpec((tokens, meta), lambda j, info: (0, width // meta)) for _ in range(4)]
    in_specs += [pl.BlockSpec((hidden, tile), lambda j, info: (0, j))]
    operands = [*shards, *shards, weight]
    if aliased:
        in_specs.append(pl.BlockSpec(memory_space=pl.ANY))
        operands.append(merged)
    return pl.pallas_call(
        functools.partial(chunk_body, experts=experts, capacity=capacity, aliased=aliased),
        grid_spec=pltpu.PrefetchScalarGridSpec(
            num_scalar_prefetch=1,
            grid=(width // tile,),
            in_specs=in_specs,
            out_specs=[
                pl.BlockSpec((rows, tile), lambda j, info: (info[1], j)),
                pl.BlockSpec((rows, hidden), lambda j, info: (0, 0)),
            ],
            scratch_shapes=[
                pltpu.VMEM((4 * tokens, rows), jnp.bfloat16),
                pltpu.VMEM((rows, LANES), jnp.float32),
                pltpu.VMEM((4 * tokens, tile), jnp.bfloat16),
                pltpu.VMEM((rows, hidden), jnp.float32),
            ],
        ),
        out_shape=[
            jax.ShapeDtypeStruct((all_rows, width), jnp.bfloat16),
            jax.ShapeDtypeStruct((rows, hidden), jnp.bfloat16),
        ],
        input_output_aliases={10: 0} if aliased else {},
        name="chunk",
    )(info, *operands)


def on_any_mesh(out_grad, gate_weight, expert_ids, replicated, down_weight, pre_act):
    devices = lax.axis_size("expert")
    half_way = devices // 2
    myself = lax.axis_index("expert")
    shares = lax.axis_size("dp")
    my_share = lax.axis_index("dp")
    tokens_here, choose = expert_ids.shape
    rows_share = pre_act.shape[2]
    all_rows = rows_share * shares
    capacity = all_rows // devices
    flat_ids = expert_ids.reshape(-1)
    experts_iota = jnp.arange(devices, dtype=jnp.int32)
    onehot = (flat_ids[:, None] == experts_iota[None, :]).astype(jnp.int32)
    position = jnp.sum(onehot * (jnp.cumsum(onehot, axis=0) - 1), axis=1)
    rep_of = jnp.sum(onehot * replicated[None, :], axis=1)
    diverted = (rep_of == 1) & (myself % 2 == 1)
    target_dev = jnp.where(diverted, (flat_ids + half_way) % devices, flat_ids)
    slot_index = diverted.astype(jnp.int32)
    target = slot_index * devices * capacity + target_dev * capacity + position
    placer = (
        jnp.arange(2 * devices * capacity, dtype=jnp.int32)[:, None] == target[None, :]
    ).astype(jnp.bfloat16)
    scaled = gate_weight[:, :, None] * out_grad.astype(jnp.float32)[:, None, :]
    routed = scaled.astype(jnp.bfloat16).reshape(tokens_here * choose, -1)
    outgoing = jnp.dot(placer, routed, preferred_element_type=jnp.float32).astype(jnp.bfloat16)
    outgoing = outgoing.reshape(2, devices, capacity, -1)
    arrived = lax.all_to_all(outgoing, "expert", split_axis=1, concat_axis=1, tiled=True).reshape(
        2, all_rows, -1
    )
    own_weight = down_weight[0]
    rep_self = jnp.sum(jnp.where(experts_iota == myself, replicated, 0))
    row_ids = my_share * rows_share + jnp.arange(rows_share, dtype=jnp.int32)
    taken_rows = (row_ids // capacity % 2 == 1) & (rep_self == 1)
    partner_rows, partner_pre = passed_along((arrived[1], pre_act[0, 1]), "expert", half_way)
    merged = arrived[0] + partner_rows
    merged_pre = jnp.where(taken_rows[:, None], partner_pre, pre_act[0, 0])
    partial_value = jnp.einsum("rd,fd->rf", merged, own_weight, preferred_element_type=jnp.float32)
    hidden = hidden_of(merged_pre)
    gradients = jnp.einsum(
        "rf,rd->fd",
        lax.all_gather(hidden, "dp", axis=0, tiled=True),
        merged,
        preferred_element_type=jnp.float32,
    )
    summed = lax.psum_scatter(
        partial_value.astype(jnp.bfloat16), "dp", scatter_dimension=0, tiled=True
    ).astype(jnp.float32)
    local_grad = swiglu_back(summed, merged_pre)
    blank_grad = jnp.zeros_like(local_grad)
    kept_grad = jnp.where(taken_rows[:, None], blank_grad, local_grad)
    sent_grad = jnp.where(taken_rows[:, None], local_grad, blank_grad)
    came_back = passed_along(sent_grad, "expert", half_way)
    grad_pre = jnp.stack([kept_grad, came_back])[None]
    grad_down = gradients.astype(jnp.bfloat16)[None]
    return (grad_down, grad_pre)


def on_device(out_grad, gate_weight, expert_ids, replicated, down_weight, pre_act):
    devices = lax.axis_size("expert")
    half_way = devices // 2
    myself = lax.axis_index("expert")
    my_share = lax.axis_index("dp")
    width = out_grad.shape[1]
    rows_share = pre_act.shape[2]
    all_rows = rows_share * lax.axis_size("dp")
    capacity = all_rows // devices
    own_weight = down_weight[0]
    hidden_width = own_weight.shape[0]
    group = 4 * capacity

    rep_self = jnp.sum(jnp.where(jnp.arange(devices) == myself, replicated, 0))
    row_ids = jnp.arange(rows_share, dtype=jnp.int32)
    odd_row = (row_ids // capacity) % 2 == 1
    taken_rows = odd_row & (rep_self == 1)

    def odd_of(rows):
        split = rows.reshape(-1, 2, capacity, rows.shape[-1])
        return split[:, 1].reshape(-1, rows.shape[-1])

    def odd_placed(rows):
        split = rows.reshape(-1, 1, capacity, rows.shape[-1])
        return jnp.concatenate([jnp.zeros_like(split), split], axis=1).reshape(-1, rows.shape[-1])

    payload = payload_of(out_grad, gate_weight, expert_ids, devices)
    column = {0: payload}
    for k in range(1, devices // 4):
        low = k & -k
        column[k] = swapped(column[k ^ low], "expert", 4 * low)

    own_hidden = hidden_of(pre_act[0, 0])
    far_hidden = hidden_of(odd_of(pre_act[0, 1]))
    partner_hidden = passed_along(far_hidden, "expert", half_way)
    hidden = jnp.where(taken_rows[:, None], odd_placed(partner_hidden), own_hidden)
    other_hidden = swapped(hidden, "dp", 1)
    first = my_share == 0
    all_hidden = jnp.concatenate(
        [jnp.where(first, hidden, other_hidden), jnp.where(first, other_hidden, hidden)], axis=0
    )

    merged = None
    partials = []
    place = myself % 4
    for k in range(devices // 4):
        mine = column[k]
        across = swapped(mine, "expert", 2)
        shards = [mine, across, swapped(mine, "expert", 1), swapped(across, "expert", 1)]
        info = jnp.stack(
            [myself, (myself // 4) ^ k]
            + [(place ^ flip) * capacity for flip in (0, 2, 1, 3)]
            + [0 * myself] * 2
        ).astype(jnp.int32)
        merged, partial_value = chunk_of(
            info, shards, own_weight, merged, devices, capacity, all_rows, 512
        )
        partials.append(partial_value)

    gradients = jnp.einsum("rf,rd->fd", all_hidden, merged, preferred_element_type=jnp.float32)

    z_index = myself // 4
    blocks = []
    owner = (z_index >> 1) == my_share
    for k in (0, 1):
        kept = jnp.where(owner, partials[k], partials[k + 2])
        sent = jnp.where(owner, partials[k + 2], partials[k])
        came = swapped(sent, "dp", 1)
        blocks.append(kept.astype(jnp.float32) + came.astype(jnp.float32))
    back = [
        passed_along(
            jnp.where(rep_self == 1, odd_of(block), 0.0).astype(jnp.bfloat16), "expert", half_way
        )
        for block in blocks
    ]
    even = (z_index & 1) == 0
    summed = jnp.concatenate(
        [jnp.where(even, blocks[0], blocks[1]), jnp.where(even, blocks[1], blocks[0])], axis=0
    )
    returned = jnp.concatenate(
        [jnp.where(even, back[0], back[1]), jnp.where(even, back[1], back[0])], axis=0
    )
    own_grad = swiglu_back(jnp.where(taken_rows[:, None], 0.0, summed), pre_act[0, 0])
    far_grad = swiglu_back(odd_placed(returned).astype(jnp.float32), pre_act[0, 1])
    grad_pre = jnp.stack([own_grad, far_grad])[None]
    return (gradients.astype(jnp.bfloat16)[None], grad_pre)


def solution(mesh):
    in_specs = (
        P("expert", "dp"),
        P("expert", None),
        P("expert", None),
        P(),
        P("expert", None, "dp"),
        P("expert", None, "dp", None),
    )
    out_specs = (P("expert", None, "dp"), P("expert", None, "dp", None))
    fits = mesh.shape["dp"] == 2 and mesh.shape["expert"] == 16
    return jax.shard_map(
        on_device if fits else on_any_mesh, mesh=mesh, in_specs=in_specs, out_specs=out_specs, check_vma=False
    )
```

```python
import functools

import jax
import jax.numpy as jnp
from jax import lax
from jax.experimental import pallas as pl
from jax.experimental.pallas import tpu as pltpu
from jax.sharding import PartitionSpec as P


LANES = 128
FIELDS = 4


def swapped(value, axis, mask):
    count = lax.axis_size(axis)
    return lax.ppermute(value, axis, [(s, s ^ mask) for s in range(count)])


def passed_along(value, axis, steps):
    count = lax.axis_size(axis)
    pairs = [(source, (source + steps) % count) for source in range(count)]
    return lax.ppermute(value, axis, pairs)


def hidden_of(stored):
    width = stored.shape[-1] // 2
    gate_part = stored[..., :width].astype(jnp.float32)
    up_part = stored[..., width:].astype(jnp.float32)
    return (gate_part * jax.nn.sigmoid(gate_part) * up_part).astype(jnp.bfloat16)


def swiglu_back(hidden_grad, stored):
    width = stored.shape[-1] // 2
    gate_part = stored[..., :width].astype(jnp.float32)
    up_part = stored[..., width:].astype(jnp.float32)
    sigmoid_v = jax.nn.sigmoid(gate_part)
    gate_grad = hidden_grad * up_part * sigmoid_v * (1.0 + gate_part * (1.0 - sigmoid_v))
    up_grad = hidden_grad * gate_part * sigmoid_v
    return jnp.concatenate([gate_grad, up_grad], axis=-1).astype(jnp.bfloat16)


def in_vmem(body, outs, operands, scratch=(), copies=0, aliases=None, limit=8 << 20, hbm_in=(), hbm_out=()):
    far = pl.BlockSpec(memory_space=pl.ANY)
    whole = pl.BlockSpec(memory_space=pltpu.VMEM)
    spaces = [far if i in hbm_in else whole for i in range(len(operands))]
    operands = [
        pltpu.with_memory_space_constraint(value, pltpu.HBM) if i in hbm_in else value
        for i, value in enumerate(operands)
    ]
    return pl.pallas_call(
        body,
        in_specs=spaces,
        out_specs=[far if i in hbm_out else whole for i in range(len(outs))],
        out_shape=[
            pltpu.HBM(shape, dtype) if i in hbm_out else jax.ShapeDtypeStruct(shape, dtype)
            for i, (shape, dtype) in enumerate(outs)
        ],
        scratch_shapes=[pltpu.VMEM(shape, dtype) for shape, dtype in scratch]
        + [pltpu.SemaphoreType.DMA((copies,))] * (copies > 0),
        input_output_aliases=aliases or {},
        compiler_params=pltpu.CompilerParams(vmem_limit_bytes=limit),
    )(*operands)


def payload_body(ids_hbm, weight_hbm, grad_hbm, out_ref, left_ref, right_ref, ids_ref, weight_ref, sems, *, experts):
    tokens, width = grad_hbm.shape
    half = width // 2
    meta = out_ref.shape[1] - width
    copies = [
        pltpu.make_async_copy(source, target, sems.at[i])
        for i, (source, target) in enumerate(
            (
                (ids_hbm, ids_ref),
                (weight_hbm, weight_ref),
                (grad_hbm, out_ref.at[:, pl.ds(0, width)]),
                (grad_hbm.at[:, pl.ds(0, half)], left_ref.at[:, pl.ds(0, half)]),
                (grad_hbm.at[:, pl.ds(half, half)], right_ref),
            )
        )
    ]
    for copy in copies:
        copy.start()
    lane = lax.broadcasted_iota(jnp.int32, (tokens, meta), 1)
    expert, field = lane % experts, lane // experts
    copies[0].wait()
    copies[1].wait()
    ids = jnp.transpose(ids_ref[...])
    weight = jnp.transpose(weight_ref[...])
    named = jnp.zeros((tokens, meta), jnp.float32)
    chosen = jnp.zeros((tokens, meta), jnp.float32)
    for k in range(ids.shape[1]):
        hit = ids[:, k : k + 1] == expert
        named = jnp.where(hit, 1.0, named)
        chosen = jnp.where(hit, weight[:, k : k + 1], chosen)
    rows = lax.broadcasted_iota(jnp.int32, (tokens, tokens), 0)
    cols = lax.broadcasted_iota(jnp.int32, (tokens, tokens), 1)
    earlier = (cols < rows).astype(jnp.bfloat16)
    position = jnp.dot(earlier, named.astype(jnp.bfloat16), preferred_element_type=jnp.float32)
    top = chosen.astype(jnp.bfloat16).astype(jnp.float32)
    mid = (chosen - top).astype(jnp.bfloat16).astype(jnp.float32)
    low = chosen - top - mid
    place = jnp.where(named > 0.0, position, -1.0)
    value = jnp.where(field == 0, place, jnp.where(field == 1, top, jnp.where(field == 2, mid, low)))
    value = jnp.where(field < FIELDS, value, 0.0).astype(jnp.bfloat16)
    out_ref[:, width:] = value
    left_ref[:, half:] = value
    for copy in copies[2:]:
        copy.wait()


def payload_of(out_grad, gate_weight, expert_ids, experts):
    tokens, width = out_grad.shape
    meta = -(-experts * FIELDS // LANES) * LANES
    top = expert_ids.shape[1]
    return in_vmem(
        functools.partial(payload_body, experts=experts),
        [((tokens, span), jnp.bfloat16) for span in (width + meta, width // 2 + meta, width // 2)],
        [expert_ids.T, gate_weight.T, out_grad],
        [((top, tokens), jnp.int32), ((top, tokens), jnp.float32)],
        copies=5,
        hbm_in=(0, 1, 2),
    )


def odd_first(rows, capacity):
    parts = [rows[i * capacity : (i + 1) * capacity] for i in (1, 3, 0, 2)]
    return jnp.concatenate(parts, axis=0)


def chunk_body(*refs, experts, capacity, flip, halves, aliased, paired, parted):
    shards, refs = refs[: 4 * halves], refs[4 * halves :]
    weight = refs[0]
    outs = refs[1 + aliased + paired :]
    merged_ref, (stack_ref, pick_ref, value_ref) = outs[0], outs[-3:]
    tokens = shards[0].shape[0]
    _, width = weight.shape
    meta = stack_ref.shape[1] - width
    rows = 4 * capacity
    myself = lax.axis_index("expert")
    place = myself % 4
    lane = lax.broadcasted_iota(jnp.int32, (tokens, meta), 1)
    row = lax.broadcasted_iota(jnp.int32, (tokens, rows), 1)
    for i, turn in enumerate((0, 2, 1, 3)):
        span = slice(i * tokens, (i + 1) * tokens)
        if halves == 1:
            stack_ref[span, :] = shards[i][...]
        else:
            left, right = shards[i], shards[4 + i]
            stack_ref[span, : width // 2] = left[:, : width // 2]
            stack_ref[span, width // 2 : width] = right[...]
            stack_ref[span, width:] = left[:, width // 2 :]
        values = stack_ref[span, width:].astype(jnp.float32)
        slot = jnp.sum(jnp.where(lane == myself, values, 0.0), axis=1, keepdims=True).astype(jnp.int32)
        target = jnp.where(slot >= 0, slot + (place ^ turn) * capacity, -1)
        pick_ref[span, :] = (target == row).astype(jnp.float32)
    pick = pick_ref[...].T.astype(jnp.bfloat16)
    chosen = jnp.dot(pick, stack_ref[...], preferred_element_type=jnp.float32)
    lane = lax.broadcasted_iota(jnp.int32, (rows, meta), 1)
    wanted = (lane % experts == myself) & (lane >= experts) & (lane < FIELDS * experts)
    scale = jnp.sum(jnp.where(wanted, chosen[:, width:], 0.0), axis=1, keepdims=True)
    merged = (scale * chosen[:, :width]).astype(jnp.bfloat16)
    merged_ref[pl.ds(((myself // 4) ^ flip) * rows, rows), :] = merged
    value = lax.dot_general(
        weight[...], merged, (((1,), (1,)), ((), ())), preferred_element_type=jnp.float32
    )
    value_ref[...] = value.T
    value = odd_first(value_ref, capacity).astype(jnp.bfloat16)
    if not paired:
        outs[1][...] = value
        return
    first = refs[1 + aliased]
    owner = (myself // 8) == lax.axis_index("dp")
    spans = [slice(0, rows // 2), slice(rows // 2, rows)] if parted else [slice(0, rows)]

    @pl.when(owner)
    def _():
        for i, span in enumerate(spans):
            outs[1 + i][...] = value[span]
        outs[1 + len(spans)][...] = first[...]

    @pl.when(jnp.logical_not(owner))
    def _():
        for i, span in enumerate(spans):
            outs[1 + i][...] = first[span, :]
        outs[1 + len(spans)][...] = value


def chunk_of(shards, weight, merged, first, experts, capacity, all_rows, flip, parted):
    tokens = shards[0].shape[0]
    hidden, width = weight.shape
    rows = 4 * capacity
    meta = -(-experts * FIELDS // LANES) * LANES
    aliased, paired = int(merged is not None), int(first is not None)
    partial = [((rows, hidden), jnp.bfloat16)]
    if paired:
        partial = [((rows // 2, hidden), jnp.bfloat16)] * 2 + partial if parted else partial * 2
    return in_vmem(
        functools.partial(
            chunk_body,
            experts=experts,
            capacity=capacity,
            flip=flip,
            halves=len(shards) // 4,
            aliased=aliased,
            paired=paired,
            parted=parted,
        ),
        [((all_rows, width), jnp.bfloat16)] + partial,
        [*shards, weight] + [merged] * aliased + [first] * paired,
        [
            ((4 * tokens, width + meta), jnp.bfloat16),
            ((4 * tokens, rows), jnp.float32),
            ((rows, hidden), jnp.float32),
        ],
        aliases={len(shards) + 1: 0} if aliased else None,
        limit=14 << 20,
    )


BAND = 48


def fetch_body(weight_hbm, stored_hbm, weight_ref, stored_ref, own_ref, far_ref, scratch_ref, sems, *, capacity):
    copies = [
        pltpu.make_async_copy(stored_hbm, stored_ref, sems.at[0]),
        pltpu.make_async_copy(weight_hbm, weight_ref, sems.at[1]),
    ]
    for copy in copies:
        copy.start()
    copies[0].wait()
    rows = stored_ref.shape[2]
    for start in range(0, rows, BAND):
        own_ref[start : start + BAND, :] = hidden_of(stored_ref[0, 0, start : start + BAND, :])
        far = hidden_of(stored_ref[0, 1, start : start + BAND, :])
        scratch_ref[start : start + BAND, :] = far.astype(jnp.float32)
    odd = [
        scratch_ref[start + capacity : start + 2 * capacity, :]
        for start in range(0, rows, 2 * capacity)
    ]
    far_ref[...] = jnp.concatenate(odd, axis=0).astype(jnp.bfloat16)
    copies[1].wait()


def flag_of(flags_ref, expert):
    flags = flags_ref[...]
    lane = lax.broadcasted_iota(jnp.int32, flags.shape, 1)
    return jnp.max(jnp.where(lane == expert, flags, 0), axis=1, keepdims=True) == 1


def down_body(
    flags_ref, mine_ref, other_ref, far_mine_ref, far_other_ref, merged_ref, out_hbm, rows_ref, turned_ref, out_ref, sems, *, capacity
):
    half, _ = mine_ref.shape
    tile = out_ref.shape[2]
    steps = merged_ref.shape[1] // tile
    taken = flag_of(flags_ref, lax.axis_index("expert"))
    share = lax.axis_index("dp")
    for which in range(2):

        @pl.when(share == which)
        def _():
            for i, (near, far) in enumerate(((mine_ref, far_mine_ref), (other_ref, far_other_ref))):
                base = (which ^ i) * half
                rows_ref[base : base + half, :] = near[...].astype(jnp.float32)
                theirs = far[...].astype(jnp.float32)
                for j in range(half // (2 * capacity)):
                    start = base + (2 * j + 1) * capacity
                    span = slice(start, start + capacity)
                    moved = theirs[j * capacity : (j + 1) * capacity]
                    rows_ref[span, :] = jnp.where(taken, moved, rows_ref[span, :])

    turned_ref[...] = rows_ref[...].T.astype(jnp.bfloat16)
    copies = []
    for j in range(steps):
        span = slice(j * tile, (j + 1) * tile)
        if j > 1:
            copies[j - 2].wait()
        out_ref[j % 2] = jnp.dot(
            turned_ref[...], merged_ref[:, span], preferred_element_type=jnp.float32
        ).astype(jnp.bfloat16)
        copies.append(
            pltpu.make_async_copy(out_ref.at[j % 2], out_hbm.at[0, :, pl.ds(j * tile, tile)], sems.at[j % 2])
        )
        copies[j].start()
    copies[-2].wait()
    copies[-1].wait()


def sum_body(flags_ref, kept_ref, came_ref, out_ref):
    rows = out_ref.shape[0]
    taken = flag_of(flags_ref, lax.axis_index("expert"))
    value = kept_ref[:rows, :].astype(jnp.float32) + came_ref[:rows, :].astype(jnp.float32)
    out_ref[...] = jnp.where(taken, value, 0.0).astype(jnp.bfloat16)


def back_into(out_ref, value_ref, stored_ref, slot, base, rows):
    for start in range(0, rows, BAND):
        span = pl.ds(pl.multiple_of(base + start, 16), BAND)
        out_ref[span, :] = swiglu_back(
            value_ref[start : start + BAND, :], stored_ref[0, slot, span, :]
        )


def own_body(flags_ref, stored_ref, kept0, came0, kept1, odd1, even1, out_hbm, out_ref, value_ref, sems, *, capacity):
    rows = 4 * capacity
    myself = lax.axis_index("expert")
    taken = flag_of(flags_ref, myself)
    copies = []
    for i, (kept, odd, even) in enumerate(
        (
            (kept0, came0[: rows // 2, :], came0[rows // 2 :, :]),
            (kept1, odd1[...], even1[...]),
        )
    ):
        base = (((myself // 4) & 1) ^ i) * rows
        odds = kept[: rows // 2, :].astype(jnp.float32) + odd.astype(jnp.float32)
        odds = jnp.where(taken, 0.0, odds)
        evens = kept[rows // 2 :, :].astype(jnp.float32) + even.astype(jnp.float32)
        for j in range(2):
            span = slice(j * capacity, (j + 1) * capacity)
            value_ref[2 * j * capacity : (2 * j + 1) * capacity, :] = evens[span]
            value_ref[(2 * j + 1) * capacity : (2 * j + 2) * capacity, :] = odds[span]
        back_into(out_ref, value_ref, stored_ref, 0, base, rows)
        span = pl.ds(pl.multiple_of(base, 16), rows)
        copies.append(pltpu.make_async_copy(out_ref.at[span], out_hbm.at[0, 0, span], sems.at[i]))
        copies[i].start()
    for copy in copies:
        copy.wait()


def far_body(stored_ref, came_ref, gradient_hbm, out_hbm, out_ref, value_ref, sems, *, capacity, pair):
    rows = 4 * capacity
    came = came_ref[...].astype(jnp.float32)
    blank = jnp.zeros((capacity, came.shape[1]), jnp.float32)
    for j in range(2):
        value_ref[2 * j * capacity : (2 * j + 1) * capacity, :] = blank
        value_ref[(2 * j + 1) * capacity : (2 * j + 2) * capacity, :] = came[
            j * capacity : (j + 1) * capacity
        ]
    base = (((lax.axis_index("expert") // 4) & 1) ^ pair) * rows
    back_into(out_ref, value_ref, stored_ref, 1, base, rows)
    span = pl.ds(pl.multiple_of(base, 16), rows)
    copy = pltpu.make_async_copy(out_ref.at[span], out_hbm.at[0, 1, span], sems.at[0])
    copy.start()
    copy.wait()


def on_any_mesh(out_grad, gate_weight, expert_ids, replicated, down_weight, pre_act):
    devices = lax.axis_size("expert")
    half_way = devices // 2
    myself = lax.axis_index("expert")
    shares = lax.axis_size("dp")
    my_share = lax.axis_index("dp")
    tokens_here, choose = expert_ids.shape
    rows_share = pre_act.shape[2]
    all_rows = rows_share * shares
    capacity = all_rows // devices
    flat_ids = expert_ids.reshape(-1)
    experts_iota = jnp.arange(devices, dtype=jnp.int32)
    onehot = (flat_ids[:, None] == experts_iota[None, :]).astype(jnp.int32)
    position = jnp.sum(onehot * (jnp.cumsum(onehot, axis=0) - 1), axis=1)
    rep_of = jnp.sum(onehot * replicated[None, :], axis=1)
    diverted = (rep_of == 1) & (myself % 2 == 1)
    target_dev = jnp.where(diverted, (flat_ids + half_way) % devices, flat_ids)
    slot_index = diverted.astype(jnp.int32)
    target = slot_index * devices * capacity + target_dev * capacity + position
    placer = (
        jnp.arange(2 * devices * capacity, dtype=jnp.int32)[:, None] == target[None, :]
    ).astype(jnp.bfloat16)
    scaled = gate_weight[:, :, None] * out_grad.astype(jnp.float32)[:, None, :]
    routed = scaled.astype(jnp.bfloat16).reshape(tokens_here * choose, -1)
    outgoing = jnp.dot(placer, routed, preferred_element_type=jnp.float32).astype(jnp.bfloat16)
    outgoing = outgoing.reshape(2, devices, capacity, -1)
    arrived = lax.all_to_all(outgoing, "expert", split_axis=1, concat_axis=1, tiled=True).reshape(
        2, all_rows, -1
    )
    own_weight = down_weight[0]
    rep_self = jnp.sum(jnp.where(experts_iota == myself, replicated, 0))
    row_ids = my_share * rows_share + jnp.arange(rows_share, dtype=jnp.int32)
    taken_rows = (row_ids // capacity % 2 == 1) & (rep_self == 1)
    partner_rows, partner_pre = passed_along((arrived[1], pre_act[0, 1]), "expert", half_way)
    merged = arrived[0] + partner_rows
    merged_pre = jnp.where(taken_rows[:, None], partner_pre, pre_act[0, 0])
    partial_value = jnp.einsum("rd,fd->rf", merged, own_weight, preferred_element_type=jnp.float32)
    hidden = hidden_of(merged_pre)
    gradients = jnp.einsum(
        "rf,rd->fd",
        lax.all_gather(hidden, "dp", axis=0, tiled=True),
        merged,
        preferred_element_type=jnp.float32,
    )
    summed = lax.psum_scatter(
        partial_value.astype(jnp.bfloat16), "dp", scatter_dimension=0, tiled=True
    ).astype(jnp.float32)
    local_grad = swiglu_back(summed, merged_pre)
    blank_grad = jnp.zeros_like(local_grad)
    kept_grad = jnp.where(taken_rows[:, None], blank_grad, local_grad)
    sent_grad = jnp.where(taken_rows[:, None], local_grad, blank_grad)
    came_back = passed_along(sent_grad, "expert", half_way)
    grad_pre = jnp.stack([kept_grad, came_back])[None]
    grad_down = gradients.astype(jnp.bfloat16)[None]
    return (grad_down, grad_pre)


def on_device(out_grad, gate_weight, expert_ids, replicated, down_weight, pre_act):
    devices = lax.axis_size("expert")
    half_way = devices // 2
    rows_share, wide = pre_act.shape[2:]
    all_rows = rows_share * lax.axis_size("dp")
    capacity = all_rows // devices
    hidden_width, width = down_weight.shape[1:]
    flags = replicated[None]
    bfloat = jnp.bfloat16
    single = jnp.float32

    payload, left, right = payload_of(out_grad, gate_weight, expert_ids, devices)
    column = {"0": payload}
    for name, base, bits in (("1", payload, 1), ("2L", left, 2), ("2R", right, 2)):
        column[name] = swapped(base, "expert", 4 * bits)
    for part in "LR":
        column["3" + part] = swapped(column["2" + part], "expert", 4)
    across, beside, corner = {}, {}, {}
    for name in column:
        across[name] = swapped(column[name], "expert", 2)
        beside[name] = swapped(column[name], "expert", 1)
        corner[name] = swapped(across[name], "expert", 1)

    own_weight, stored, own_hidden, far_hidden = in_vmem(
        functools.partial(fetch_body, capacity=capacity),
        [
            ((hidden_width, width), bfloat),
            (pre_act.shape, bfloat),
            ((rows_share, wide // 2), bfloat),
            ((rows_share // 2, wide // 2), bfloat),
        ],
        [down_weight[0], pre_act],
        [((rows_share, wide // 2), single)],
        copies=2,
        hbm_in=(0, 1),
    )
    other_hidden = swapped(own_hidden, "dp", 1)
    far_mine = passed_along(far_hidden, "expert", half_way)
    far_other = swapped(far_mine, "dp", 1)

    def chunk(k, names, merged, first, parted=False):
        shards = [group[name] for name in names for group in (column, across, beside, corner)]
        return chunk_of(
            shards, own_weight, merged, first, devices, capacity, all_rows, k, parted
        )

    merged, first0 = chunk(0, ("0",), None, None)
    merged, first1 = chunk(1, ("1",), merged, None)
    merged, sent0, kept0 = chunk(2, ("2L", "2R"), merged, first0)
    merged, odd1, even1, kept1 = chunk(3, ("3L", "3R"), merged, first1, parted=True)
    came = {}
    for name, value in (("r0", sent0), ("r1o", odd1), ("r1e", even1)):
        came[name] = swapped(value, "dp", 1)
    back = []
    for kept, arrived in ((kept0, came["r0"]), (kept1, came["r1o"])):
        outgoing = in_vmem(sum_body, [((2 * capacity, hidden_width), bfloat)], [flags, kept, arrived])[0]
        back.append(passed_along(outgoing, "expert", half_way))

    tile = 512
    gradients = in_vmem(
        functools.partial(down_body, capacity=capacity),
        [((1, hidden_width, width), bfloat)],
        [flags, own_hidden, other_hidden, far_mine, far_other, merged],
        [
            ((all_rows, hidden_width), single),
            ((hidden_width, all_rows), bfloat),
            ((2, hidden_width, tile), bfloat),
        ],
        copies=2,
        hbm_out=(0,),
        limit=14 << 20,
    )[0]
    grad_pre = in_vmem(
        functools.partial(own_body, capacity=capacity),
        [(pre_act.shape, bfloat)],
        [flags, stored, kept0, came["r0"], kept1, came["r1o"], came["r1e"]],
        [((rows_share, wide), bfloat), ((4 * capacity, wide // 2), single)],
        copies=2,
        hbm_out=(0,),
    )[0]
    for i in range(2):
        grad_pre = in_vmem(
            functools.partial(far_body, capacity=capacity, pair=i),
            [(pre_act.shape, bfloat)],
            [stored, back[i], grad_pre],
            [((rows_share, wide), bfloat), ((4 * capacity, wide // 2), single)],
            copies=1,
            aliases={2: 0},
            hbm_in=(2,),
            hbm_out=(0,),
        )[0]
    return (gradients, grad_pre)


def solution(mesh):
    in_specs = (
        P("expert", "dp"),
        P("expert", None),
        P("expert", None),
        P(),
        P("expert", None, "dp"),
        P("expert", None, "dp", None),
    )
    out_specs = (P("expert", None, "dp"), P("expert", None, "dp", None))
    fits = mesh.shape["dp"] == 2 and mesh.shape["expert"] == 16
    return jax.shard_map(
        on_device if fits else on_any_mesh,
        mesh=mesh,
        in_specs=in_specs,
        out_specs=out_specs,
        check_vma=False,
    )
```
